32 devices in a mesh: pb: 8 (over y, x, core), pa: 4 (over z).
Axes of the slice: x: 2, y: 2, z: 4, core: 2. Of those that a mesh axis runs over, the one named last changes fastest.
Arguments:
- queries: bfloat16 [2048, 128], P('pb'), may hold values from -10.5 to 10.5, as said below
- encoder_outputs: bfloat16 [8, 64, 128, 1024], P('pb', 'pa'), may hold values from -6 to 6
- proj_weight: bfloat16 [1024, 128], replicated, may hold values from -0.1875 to 0.1875
- bm25_rank: int32 [64, 4, 64], P('pb', 'pa'), may hold values from 0 to 199
- dense_rank: int32 [64, 4, 64], P('pb', 'pa'), may hold values from 0 to 199
- custodian_document_index: int32 [8, 64], P('pb', 'pa'), may hold values from -1 to 31, as said below
Outputs:
- query_grad: float32 [2048, 128], P(('pb', 'pa'))
- encoder_output_derivative: bfloat16 [8, 64, 128, 1024], P('pb', 'pa')
The draws below stay inside these ranges and needn't reach their ends.
Inputs may be any that keep to these rules, and one draw needn't show every extreme that they name: `queries`: A custom draw: each entry lies between the bounds; rows may differ in scale. `custodian_document_index`: within each row b every number n from 0 to 31 appears exactly once and stands for passage (n // 8, b * 8 + n % 8); all other entries are -1. The owner of columns o * 16 to o * 16 + 15 is index o of pa; an owner holds 0, 8 or 16 passages, and at most 4 with the same n // 8. Some owner is full and some owner holds exactly 4 passages with the same n // 8 in every row.
All inputs are finite; a program needn't handle non-finite values.
Results may differ from the reference program's by a relative error of at most 0.025.
The reference program's roundings to bfloat16 on the way count: a program that leaves them out, or rounds other values in their place, can miss the bound.
Values may be sent and summed in bfloat16 or wider, within the bound.
A program may use at most 64 MiB of HBM per device.

```python
import jax
import jax.numpy as jnp
from jax import lax

DIM = 128
H = 1024
QT = 32
LEN = 128
PD = 8
DEPTH = 100
Q = 64
M = 64
CAP = 16
N_PB = 8
N_PA = 4


def draw_queries(key, part):
    shape = (Q * QT, DIM)
    values = 0.25 * jax.random.normal(key, shape, jnp.float32)
    return jnp.clip(values, -1.5, 1.5).astype(jnp.bfloat16)


def owner_group(key):
    order_key, slot_key = jax.random.split(jax.random.fold_in(key, 7))
    owner_order = jax.random.permutation(order_key, N_PA)
    owner_rank = jnp.argsort(owner_order).astype(jnp.int32)
    quarter = N_PA // 4
    load = jnp.where(owner_rank < quarter, 2 * PD, jnp.where(owner_rank < 3 * quarter, PD, 0))
    begin = 2 * PD * jnp.minimum(owner_rank, quarter) + PD * jnp.clip(owner_rank - quarter, 0, 2 * quarter)
    shuffles = jax.vmap(lambda one_key: jax.random.permutation(one_key, CAP))(jax.random.split(slot_key, N_PA))
    listed = begin[:, None] + shuffles
    scorer = listed % N_PA
    within = listed // N_PA
    filled = jnp.where(shuffles < load[:, None], scorer * PD + within, -1)
    return filled.reshape(N_PA * CAP).astype(jnp.int32)


def draw_custodian_document_index(key, part):
    group_keys = jax.random.split(jax.random.fold_in(key, 11), N_PB)
    return jax.vmap(owner_group)(group_keys)


def touch_ends(values, key, least, top_value):
    extent = values.shape
    index_at = [jax.random.randint(jax.random.fold_in(key, axis), (), 0, extent[axis]) for axis in range(len(extent))]
    values = values.at[tuple(index_at)].set(least)
    longest = extent.index(max(extent))
    index_at[longest] = (index_at[longest] + 1) % extent[longest]
    return values.at[tuple(index_at)].set(top_value)


def level_of(stream_key, dims, shards, least, high):
    factor_of = 1.0
    for position, shards_of in shards:
        steps = jax.random.uniform(jax.random.fold_in(jax.random.fold_in(stream_key, 6), position), (shards_of,), jnp.float32, least / len(shards), high / len(shards))
        factor_of = factor_of * jnp.repeat(jnp.exp(steps), dims[position] // shards_of).reshape((-1,) + (1,) * (len(dims) - 1 - position))
    return factor_of


def gaussian(rng, shape, spread, most, cuts=(), kind=jnp.bfloat16):
    array = jax.random.normal(rng, shape, jnp.float32) * spread
    if len(cuts) > 0:
        array = level_of(rng, shape, cuts, -0.22, 0.18) * array
    return jnp.clip(array, min=-most, max=most).astype(kind)


def setup_inputs(seed: int = 0) -> dict:
    splits = jax.random.split(jax.random.key(seed), 7)
    return {
        "queries": draw_queries(jax.random.fold_in(splits[6], 71), 0),
        "encoder_outputs": gaussian(splits[1], (N_PB, N_PA * CAP, LEN, H), 1.0, 6.0, ((0, 8), (1, 4))),
        "proj_weight": gaussian(splits[2], (H, DIM), H ** -0.5, 0.1875),
        "bm25_rank": touch_ends(jax.random.randint(splits[3], (Q, N_PA, M), 0, 2 * DEPTH), jax.random.fold_in(splits[3], 1), 0, (2 * DEPTH) - 1).astype(jnp.int32),
        "dense_rank": touch_ends(jax.random.randint(splits[4], (Q, N_PA, M), 0, 2 * DEPTH), jax.random.fold_in(splits[4], 1), 0, (2 * DEPTH) - 1).astype(jnp.int32),
        "custodian_document_index": draw_custodian_document_index(jax.random.fold_in(splits[6], 71), 0),
    }


tau = 0.05
inv_temp = 20.0
rrf_offset = 60.0
norm_eps = 1e-06

def normalize(hid_rows, weight):
    projected = jnp.dot(hid_rows, weight, preferred_element_type=jnp.float32)
    scaling = lax.rsqrt(lax.optimization_barrier(jnp.sum(projected * projected, axis=-1, keepdims=True)) + norm_eps)
    return (projected * scaling, scaling)

def joined_target(bm25_rank, dense_rank):
    first = jnp.where(bm25_rank < DEPTH, rrf_offset / (rrf_offset + bm25_rank.astype(jnp.float32)), 0.0)
    second = jnp.where(dense_rank < DEPTH, rrf_offset / (rrf_offset + dense_rank.astype(jnp.float32)), 0.0)
    return (first + second).astype(jnp.float32)

def similarity(query_rows, key_block):
    flat_keys = key_block.reshape(PD * LEN, DIM)
    raw = jnp.dot(query_rows, flat_keys.T, preferred_element_type=jnp.float32) * inv_temp
    return raw.reshape(query_rows.shape[0], PD, LEN)

def log_total(raw):
    largest = lax.optimization_barrier(jnp.max(raw, axis=2, keepdims=True))
    return largest[:, :, 0] + jnp.log(lax.optimization_barrier(jnp.sum(jnp.exp(raw - largest), axis=2)))

def reference(queries, encoder_outputs, proj_weight, bm25_rank, dense_rank, custodian_document_index):
    holders = N_PA * PD
    blocks_all = N_PA * N_PB

    def embedding_cluster(packed):
        hid_group, slot_ids = packed
        unit_rows, scaling = normalize(hid_group.reshape(-1, H), proj_weight)
        emb_rows = unit_rows.astype(jnp.bfloat16).reshape(N_PA * CAP, LEN, DIM)
        target_at = jnp.where(slot_ids >= 0, slot_ids, holders).astype(jnp.int32)
        positioned_rows = jnp.zeros((holders, LEN, DIM), jnp.bfloat16).at[target_at].set(emb_rows, mode='drop')
        return (unit_rows, scaling, positioned_rows)
    task_portions, multiplier_list, positioned_rows = lax.map(embedding_cluster, (encoder_outputs, custodian_document_index))
    key_blocks = positioned_rows.reshape(N_PB, N_PA, PD, LEN, DIM).transpose(1, 0, 2, 3, 4)
    key_blocks = key_blocks.reshape(blocks_all, PD, LEN, DIM)
    lse_blocks = lax.map(lambda key_block: log_total(similarity(queries, key_block)), key_blocks)
    score = lse_blocks.reshape(blocks_all, Q, QT, PD).sum(axis=2) * (tau / QT)
    score = score.reshape(N_PA, N_PB, Q, PD).transpose(2, 0, 1, 3).reshape(Q, N_PA, M)
    residual = (score - joined_target(bm25_rank, dense_rank)).astype(jnp.bfloat16)
    residual_blocks = residual.astype(jnp.float32).reshape(Q, N_PA, N_PB, PD).transpose(1, 2, 0, 3)
    residual_blocks = residual_blocks.reshape(blocks_all, Q, PD)

    def backward_block(query_acc, packed):
        key_block, lse_block, residual_block = packed
        raw = similarity(queries, key_block)
        weights = jnp.exp(raw - lse_block[:, :, None])
        per_row = jnp.repeat(residual_block, QT, axis=0)
        coefficient = ((per_row / QT)[:, :, None] * weights).astype(jnp.bfloat16).reshape(Q * QT, PD * LEN)
        query_acc = query_acc + jnp.dot(coefficient, key_block.reshape(PD * LEN, DIM), preferred_element_type=jnp.float32)
        emb_part = jnp.dot(coefficient.T, queries, preferred_element_type=jnp.float32)
        return (query_acc, emb_part.astype(jnp.bfloat16))
    query_grad, emb_grad = lax.scan(backward_block, jnp.zeros((Q * QT, DIM), jnp.float32), (key_blocks, lse_blocks, residual_blocks))
    vector_groupings = emb_grad.reshape(N_PA, N_PB, PD, LEN, DIM).transpose(1, 0, 2, 3, 4).reshape(N_PB, holders, LEN, DIM)

    def custodian_reverse_traversal(packed):
        slot_ids, unit_rows, scaling, grads_group = packed
        filled = slot_ids >= 0
        picked = jnp.take(grads_group, jnp.clip(slot_ids, 0, holders - 1).astype(jnp.int32), axis=0)
        picked = jnp.where(filled[:, None, None], picked, jnp.zeros((), jnp.bfloat16))
        slot_grad = picked.astype(jnp.float32).reshape(-1, DIM)
        inner = lax.optimization_barrier(jnp.sum(unit_rows * slot_grad, axis=-1, keepdims=True))
        proj_grad = ((slot_grad - unit_rows * inner) * scaling).astype(jnp.bfloat16)
        hid_grad = jnp.dot(proj_grad, proj_weight.T, preferred_element_type=jnp.float32).astype(jnp.bfloat16)
        return hid_grad.reshape(N_PA * CAP, LEN, H)
    encoder_output_derivative = lax.map(custodian_reverse_traversal, (custodian_document_index, task_portions, multiplier_list, vector_groupings))
    return (query_grad, encoder_output_derivative)
```

```python
import functools
import math

import jax
import jax.numpy as jnp
from jax import lax
from jax.experimental import pallas as pl
from jax.experimental.pallas import tpu as pltpu
from jax.sharding import PartitionSpec as P

DEPTH = 100

tau = 0.05
inv_temp = 20.0
rrf_offset = 60.0
norm_eps = 1e-06

MESH = pl.DeviceIdType.MESH
F32 = jnp.float32
BF16 = jnp.bfloat16


def joined_target(bm25_rank, dense_rank):
    first = jnp.where(bm25_rank < DEPTH, rrf_offset / (rrf_offset + bm25_rank.astype(F32)), 0.0)
    second = jnp.where(dense_rank < DEPTH, rrf_offset / (rrf_offset + dense_rank.astype(F32)), 0.0)
    return first + second


def xor(a, b, size):
    total = 0
    bit = 1
    while bit < size:
        total = total + ((a // bit + b // bit) % 2) * bit
        bit *= 2
    return total


def three_parts(x):
    first = x.astype(BF16)
    rest = x - first.astype(F32)
    second = rest.astype(BF16)
    third = (rest - second.astype(F32)).astype(BF16)
    return first, second, third


def nt_dot(a, b):
    return lax.dot_general(a, b, (((1,), (1,)), ((), ())), preferred_element_type=F32)


def nn_dot(a, b):
    return jnp.dot(a, b, preferred_element_type=F32)


def step_kernel(
    n_pb, n_pa, slots, length, pd, tokens,
    q_ref, x_ref, w_ref, bm_ref, de_ref, idx_ref,
    pg_ref, qg_ref,
    x_buf, unit, scale, emb, emb_t, prob, coef, emb_acc, lse_buf, inv_buf,
    q_buf, t_buf, t_exp, dq_own, dq_out, dq_in, sum_out, sum_in,
    x_sem, q_send, q_recv, t_send, t_recv, u_send, u_recv, d_send, d_recv, s_send, s_recv,
):
    b = lax.axis_index("pb")
    o = lax.axis_index("pa")
    rows = q_ref.shape[0]
    q_count, m_all = bm_ref.shape
    piece = rows // n_pa

    def x_copy(k):
        part = pl.ds(k * length, length)
        return pltpu.make_async_copy(x_ref.at[part], x_buf.at[part], x_sem.at[k])

    def q_copy(d):
        return pltpu.make_async_remote_copy(
            q_ref, q_buf.at[d], q_send.at[d], q_recv.at[d],
            device_id={"pb": xor(b, d, n_pb)}, device_id_type=MESH)

    def t_copy(d):
        return pltpu.make_async_remote_copy(
            t_buf.at[0, 0], t_buf.at[0, d], t_send.at[d], t_recv.at[d],
            device_id={"pb": xor(b, d, n_pb)}, device_id_type=MESH)

    def u_copy(e):
        return pltpu.make_async_remote_copy(
            t_buf.at[0], t_buf.at[e], u_send.at[e], u_recv.at[e],
            device_id={"pa": (o + e) % n_pa}, device_id_type=MESH)

    def d_copy(d):
        return pltpu.make_async_remote_copy(
            dq_out.at[d], dq_in.at[d], d_send.at[d], d_recv.at[d],
            device_id={"pb": xor(b, d, n_pb)}, device_id_type=MESH)

    def s_copy(e):
        to = (o + e) % n_pa
        return pltpu.make_async_remote_copy(
            sum_out.at[pl.ds(pl.multiple_of(to * piece, piece), piece)],
            sum_in.at[e], s_send.at[e], s_recv.at[e],
            device_id={"pa": to}, device_id_type=MESH)

    for k in range(slots):
        x_copy(k).start()

    barrier = pltpu.get_barrier_semaphore()
    for d in range(1, n_pb):
        pl.semaphore_signal(barrier, inc=1, device_id={"pb": xor(b, d, n_pb)}, device_id_type=MESH)
    for e in range(1, n_pa):
        pl.semaphore_signal(barrier, inc=1, device_id={"pa": (o + e) % n_pa}, device_id_type=MESH)

    t_buf[0, 0, :, 0:m_all] = joined_target(bm_ref[...], de_ref[...])
    q_buf[0] = q_ref[...]

    pl.semaphore_wait(barrier, n_pb + n_pa - 2)
    for d in range(1, n_pb):
        t_copy(d).start()
    for d in range(n_pb - 1, 0, -1):
        q_copy(d).start()

    for k in range(slots):
        x_copy(k).wait()
        part = pl.ds(k * length, length)
        projected = nn_dot(x_buf[part, :], w_ref[...])
        scaling = lax.rsqrt(jnp.sum(projected * projected, axis=1, keepdims=True) + norm_eps)
        unit_k = projected * scaling
        unit[part, :] = unit_k
        scale[part, :] = scaling
        emb[part, :] = unit_k.astype(BF16)
        emb_t[:, part] = jnp.transpose(unit_k).astype(BF16)
        if k == slots // 2:
            for d in range(1, n_pb):
                t_copy(d).wait_recv()
            for e in range(1, n_pa):
                u_copy(e).start()
    emb_acc[...] = jnp.zeros_like(emb_acc)

    for e in range(1, n_pa):
        u_copy(e).wait_recv()
    across = jnp.broadcast_to(idx_ref[...], (slots, slots))
    on_diagonal = lax.broadcasted_iota(jnp.int32, (slots, slots), 0) == lax.broadcasted_iota(
        jnp.int32, (slots, slots), 1)
    held = jnp.sum(jnp.where(on_diagonal, across, 0).astype(F32), axis=1, keepdims=True)
    held = held.astype(jnp.int32)
    filled = held >= 0
    column = lax.broadcasted_iota(jnp.int32, (slots, m_all), 1)
    picked = jnp.zeros((slots, n_pb * q_count), F32)
    for e in range(n_pa):
        shard = (o - e + n_pa) % n_pa
        one_hot = (held == column + (shard - b) * pd) & (column >= b * pd) & (column < (b + 1) * pd)
        one_hot = jnp.where(one_hot, 1.0, 0.0).astype(BF16)
        table = t_buf[e, :, :, 0:m_all].reshape(n_pb * q_count, m_all)
        for part in three_parts(table):
            picked = picked + nt_dot(one_hot, part)
    picked_parts = jnp.concatenate([p.astype(F32) for p in three_parts(picked)], axis=0).astype(BF16)
    for d in range(n_pb):
        row_at = lax.broadcasted_iota(jnp.int32, (n_pb * q_count, rows), 0)
        lane_at = lax.broadcasted_iota(jnp.int32, (n_pb * q_count, rows), 1)
        spread = jnp.where(row_at == d * q_count + lane_at // tokens, 1.0, 0.0).astype(BF16)
        wide = nn_dot(picked_parts, spread)
        t_exp[d] = wide[0:slots] + wide[slots:2 * slots] + wide[2 * slots:3 * slots]

    same_query = jnp.where(
        lax.broadcasted_iota(jnp.int32, (rows, rows), 0) // tokens
        == lax.broadcasted_iota(jnp.int32, (rows, rows), 1) // tokens, 1.0, 0.0).astype(BF16)

    def one_group(turn, carry):
        d = n_pb - 1 - turn

        @pl.when(d > 0)
        def _():
            q_copy(d).wait_recv()

        q_rows = q_buf[d]
        for k in range(slots):
            part = pl.ds(k * length, length)
            raw = nt_dot(emb[part, :], q_rows)
            largest = jnp.max(raw, axis=0, keepdims=True)
            power = jnp.exp2((raw - largest) * (inv_temp * math.log2(math.e)))
            total = jnp.sum(power, axis=0, keepdims=True)
            prob[part, :] = power
            lse_buf[pl.ds(k, 1), :] = largest * inv_temp + jnp.log(total)
            inv_buf[pl.ds(k, 1), :] = 1.0 / total
        first, second, third = three_parts(lse_buf[...])
        score = nn_dot(first, same_query) + nn_dot(second, same_query) + nn_dot(third, same_query)
        score = score * (tau / tokens)
        residual = (score - t_exp[d]).astype(BF16).astype(F32)
        factor = jnp.where(filled, residual * (1.0 / tokens) * inv_buf[...], 0.0)
        for k in range(slots):
            part = pl.ds(k * length, length)
            c = (prob[part, :] * factor[k:k + 1, :]).astype(BF16)
            coef[part, :] = c
            emb_acc[part, :] += nn_dot(c, q_rows)
        dq = nn_dot(emb_t[...], coef[...])
        dq_own[...] = dq
        dq_out[d] = dq.astype(BF16)

        @pl.when(d > 0)
        def _():
            d_copy(d).start()

        return carry

    lax.fori_loop(0, n_pb, one_group, 0)

    total = dq_own[...]
    for d in range(n_pb - 1, 0, -1):
        d_copy(d).wait_recv()
        total = total + dq_in[d].astype(F32)
    summed = jnp.transpose(total)
    dq_rows = summed
    sum_out[...] = dq_rows.astype(BF16)
    for e in range(1, n_pa):
        s_copy(e).start()

    for k in range(slots):
        part = pl.ds(k * length, length)
        slot_grad = emb_acc[part, :].astype(BF16).astype(F32)
        unit_k = unit[part, :]
        inner = jnp.sum(unit_k * slot_grad, axis=1, keepdims=True)
        pg_ref[part, :] = ((slot_grad - unit_k * inner) * scale[part, :]).astype(BF16)

    mine = sum_out[pl.ds(pl.multiple_of(o * piece, piece), piece), :].astype(F32)
    for e in range(1, n_pa):
        s_copy(e).wait_recv()
        mine = mine + sum_in[e].astype(F32)
    qg_ref[...] = mine

    for d in range(1, n_pb):
        t_copy(d).wait_send()
        q_copy(d).wait_send()
        d_copy(d).wait_send()
    for e in range(1, n_pa):
        u_copy(e).wait_send()
        s_copy(e).wait_send()


def solution(mesh):
    n_pb, n_pa = mesh.shape["pb"], mesh.shape["pa"]

    def on_device(queries, encoder_outputs, proj_weight, bm25_rank, dense_rank, custodian):
        _, slots, length, hidden = encoder_outputs.shape
        dim = proj_weight.shape[1]
        rows = queries.shape[0]
        q_count, _, m_all = bm25_rank.shape
        pd = m_all // n_pb
        tokens = rows // q_count
        all_rows = slots * length
        piece = rows // n_pa
        vmem = pl.BlockSpec(memory_space=pltpu.VMEM)
        dma = pltpu.SemaphoreType.DMA
        proj_grad, query_grad = pl.pallas_call(
            functools.partial(step_kernel, n_pb, n_pa, slots, length, pd, tokens),
            out_shape=(
                jax.ShapeDtypeStruct((all_rows, dim), BF16),
                jax.ShapeDtypeStruct((piece, dim), F32),
            ),
            in_specs=[vmem, pl.BlockSpec(memory_space=pl.ANY), vmem, vmem, vmem, vmem],
            out_specs=(vmem, vmem),
            scratch_shapes=[
                pltpu.VMEM((all_rows, hidden), BF16),
                pltpu.VMEM((all_rows, dim), F32),
                pltpu.VMEM((all_rows, 1), F32),
                pltpu.VMEM((all_rows, dim), BF16),
                pltpu.VMEM((dim, all_rows), BF16),
                pltpu.VMEM((all_rows, rows), F32),
                pltpu.VMEM((all_rows, rows), BF16),
                pltpu.VMEM((all_rows, dim), F32),
                pltpu.VMEM((slots, rows), F32),
                pltpu.VMEM((slots, rows), F32),
                pltpu.VMEM((n_pb, rows, dim), BF16),
                pltpu.VMEM((n_pa, n_pb, q_count, max(128, m_all)), F32),
                pltpu.VMEM((n_pb, slots, rows), F32),
                pltpu.VMEM((dim, rows), F32),
                pltpu.VMEM((n_pb, dim, rows), BF16),
                pltpu.VMEM((n_pb, dim, rows), BF16),
                pltpu.VMEM((rows, dim), BF16),
                pltpu.VMEM((n_pa, piece, dim), BF16),
                dma((slots,)),
                dma((n_pb,)), dma((n_pb,)),
                dma((n_pb,)), dma((n_pb,)),
                dma((n_pa,)), dma((n_pa,)),
                dma((n_pb,)), dma((n_pb,)),
                dma((n_pa,)), dma((n_pa,)),
            ],
            compiler_params=pltpu.CompilerParams(collective_id=0, has_side_effects=True),
        )(
            queries, encoder_outputs.reshape(all_rows, hidden), proj_weight,
            bm25_rank[:, 0, :], dense_rank[:, 0, :], custodian,
        )
        hid_grad = lax.dot_general(
            proj_grad, proj_weight, (((1,), (1,)), ((), ())), preferred_element_type=F32)
        return query_grad, hid_grad.astype(BF16).reshape(1, slots, length, hidden)

    return jax.shard_map(
        on_device,
        mesh=mesh,
        in_specs=(
            P("pb", None),
            P("pb", "pa", None, None),
            P(),
            P("pb", "pa", None),
            P("pb", "pa", None),
            P("pb", "pa"),
        ),
        out_specs=(P(("pb", "pa"), None), P("pb", "pa", None, None)),
        check_vma=False,
    )
```

```python
import functools
import math

import jax
import jax.numpy as jnp
from jax import lax
from jax.experimental import pallas as pl
from jax.experimental.pallas import tpu as pltpu
from jax.sharding import PartitionSpec as P

DEPTH = 100

tau = 0.05
inv_temp = 20.0
rrf_offset = 60.0
norm_eps = 1e-06

MESH = pl.DeviceIdType.MESH
F32 = jnp.float32
BF16 = jnp.bfloat16


def joined_target(bm25_rank, dense_rank):
    first = jnp.where(bm25_rank < DEPTH, rrf_offset / (rrf_offset + bm25_rank.astype(F32)), 0.0)
    second = jnp.where(dense_rank < DEPTH, rrf_offset / (rrf_offset + dense_rank.astype(F32)), 0.0)
    return first + second


def xor(a, b, size):
    total = 0
    bit = 1
    while bit < size:
        total = total + ((a // bit + b // bit) % 2) * bit
        bit *= 2
    return total


def three_parts(x):
    first = x.astype(BF16)
    rest = x - first.astype(F32)
    second = rest.astype(BF16)
    third = (rest - second.astype(F32)).astype(BF16)
    return first, second, third


def nt_dot(a, b):
    return lax.dot_general(a, b, (((1,), (1,)), ((), ())), preferred_element_type=F32)


def nn_dot(a, b):
    return jnp.dot(a, b, preferred_element_type=F32)


def step_kernel(
    n_pb, n_pa, slots, length, pd, tokens,
    q_ref, x_ref, w_ref, bm_ref, de_ref, idx_ref,
    pg_ref, qg_ref,
    x_buf, w_buf, bm_buf, de_buf, idx_buf,
    unit, scale, emb, emb_t, prob_a, prob_b, coef, lse_a, lse_b, inv_a, inv_b,
    q_buf, t_buf, t_exp, dq_own, dq_out, dq_in, sum_out, sum_in,
    x_sem, i_sem, q_send, q_recv, t_send, t_recv, u_send, u_recv, d_send, d_recv, s_send, s_recv,
):
    b = lax.axis_index("pb")
    o = lax.axis_index("pa")
    rows = q_ref.shape[0]
    q_count, m_all = bm_ref.shape
    piece = rows // n_pa
    chunk = 4 if slots % 4 == 0 else 1

    def x_copy(k):
        part = pl.ds(k * length, length)
        return pltpu.make_async_copy(x_ref.at[part], x_buf.at[part], x_sem.at[k])

    def q_copy(d):
        return pltpu.make_async_remote_copy(
            q_buf.at[0], q_buf.at[d], q_send.at[d], q_recv.at[d],
            device_id={"pb": xor(b, d, n_pb)}, device_id_type=MESH)

    def t_copy(d):
        return pltpu.make_async_remote_copy(
            t_buf.at[0, 0], t_buf.at[0, d], t_send.at[d], t_recv.at[d],
            device_id={"pb": xor(b, d, n_pb)}, device_id_type=MESH)

    def u_copy(e):
        return pltpu.make_async_remote_copy(
            t_buf.at[0], t_buf.at[e], u_send.at[e], u_recv.at[e],
            device_id={"pa": (o + e) % n_pa}, device_id_type=MESH)

    def d_copy(d):
        return pltpu.make_async_remote_copy(
            dq_out.at[d], dq_in.at[d], d_send.at[d], d_recv.at[d],
            device_id={"pb": xor(b, d, n_pb)}, device_id_type=MESH)

    def s_copy(e):
        to = (o + e) % n_pa
        return pltpu.make_async_remote_copy(
            sum_out.at[pl.ds(pl.multiple_of(to * piece, piece), piece)],
            sum_in.at[e], s_send.at[e], s_recv.at[e],
            device_id={"pa": to}, device_id_type=MESH)

    barrier = pltpu.get_barrier_semaphore()
    for d in range(1, n_pb):
        pl.semaphore_signal(barrier, inc=1, device_id={"pb": xor(b, d, n_pb)}, device_id_type=MESH)
    for e in range(1, n_pa):
        pl.semaphore_signal(barrier, inc=1, device_id={"pa": (o + e) % n_pa}, device_id_type=MESH)

    small = [
        pltpu.make_async_copy(src, dst, i_sem.at[n])
        for n, (src, dst) in enumerate((
            (w_ref, w_buf), (q_ref, q_buf.at[0]), (bm_ref, bm_buf), (de_ref, de_buf),
            (idx_ref, idx_buf)))
    ]
    small[2].start()
    small[3].start()
    small[0].start()
    for k in range(slots):
        x_copy(k).start()
        if k == chunk - 1:
            small[1].start()
            small[4].start()

    def project(c):
        part = pl.ds(c * chunk * length, chunk * length)
        for k in range(c * chunk, (c + 1) * chunk):
            x_copy(k).wait()
        projected = nn_dot(x_buf[part, :], w_buf[...])
        scaling = lax.rsqrt(jnp.sum(projected * projected, axis=1, keepdims=True) + norm_eps)
        unit_c = projected * scaling
        unit[part, :] = unit_c
        scale[part, :] = scaling
        emb[part, :] = unit_c.astype(BF16)
        emb_t[:, part] = jnp.transpose(unit_c).astype(BF16)

    def send_first():
        pl.semaphore_wait(barrier, n_pb + n_pa - 2)
        for d in range(1, n_pb):
            t_copy(d).start()
        for d in range(n_pb - 1, 0, -1):
            q_copy(d).start()

    def send_second():
        for d in range(1, n_pb):
            t_copy(d).wait_recv()
        for e in range(1, n_pa):
            u_copy(e).start()

    small[2].wait()
    small[3].wait()
    t_buf[0, 0, :, 0:m_all] = joined_target(bm_buf[...], de_buf[...])
    small[0].wait()
    chunks = slots // chunk
    first_at = (chunks - 1) // 2
    second_at = chunks - 1
    for c in range(chunks):
        project(c)
        if c == first_at:
            small[1].wait()
            small[4].wait()
            send_first()
        if c == second_at:
            send_second()

    same_query = jnp.where(
        lax.broadcasted_iota(jnp.int32, (rows, rows), 0) // tokens
        == lax.broadcasted_iota(jnp.int32, (rows, rows), 1) // tokens, 1.0, 0.0).astype(BF16)
    across = jnp.broadcast_to(idx_buf[...], (slots, slots))
    on_diagonal = lax.broadcasted_iota(jnp.int32, (slots, slots), 0) == lax.broadcasted_iota(
        jnp.int32, (slots, slots), 1)
    held = jnp.sum(jnp.where(on_diagonal, across, 0).astype(F32), axis=1, keepdims=True)
    held = held.astype(jnp.int32)
    filled = held >= 0

    def score_slot(k, q_rows, prob, lse, inv):
        part = pl.ds(k * length, length)
        raw = nt_dot(emb[part, :], q_rows)
        largest = jnp.max(raw, axis=0, keepdims=True)
        power = jnp.exp2((raw - largest) * (inv_temp * math.log2(math.e)))
        total = jnp.sum(power, axis=0, keepdims=True)
        prob[part, :] = power
        lse[pl.ds(k, 1), :] = largest * inv_temp + jnp.log(total)
        inv[pl.ds(k, 1), :] = 1.0 / total

    def factor_of(d, lse, inv):
        first, second, third = three_parts(lse[...])
        score = nn_dot(first, same_query) + nn_dot(second, same_query) + nn_dot(third, same_query)
        residual = (score * (tau / tokens) - t_exp[d]).astype(BF16).astype(F32)
        return jnp.where(filled, residual * (1.0 / tokens) * inv[...], 0.0)

    def grad_slot(k, d, factor, prob):
        part = pl.ds(k * length, length)
        lanes = pl.ds(pl.multiple_of(d * rows, rows), rows)
        coef[part, lanes] = (prob[part, :] * factor[k:k + 1, :]).astype(BF16)

    def query_grad(d):
        lanes = pl.ds(pl.multiple_of(d * rows, rows), rows)
        return nn_dot(emb_t[...], coef[:, lanes])

    def send_grad(d):
        dq_out[d] = query_grad(d).astype(BF16)
        d_copy(d).start()

    buf_a = (prob_a, lse_a, inv_a)
    buf_b = (prob_b, lse_b, inv_b)

    def beside(d_new, new, d_old, old):
        q_copy(d_new).wait_recv()
        q_rows = q_buf[d_new]
        factor = factor_of(d_old, old[1], old[2])
        for k in range(slots):
            score_slot(k, q_rows, *new)
            if k > 0:
                grad_slot(k - 1, d_old, factor, old[0])
        grad_slot(slots - 1, d_old, factor, old[0])

    q_own = q_buf[0]
    for k in range(slots):
        score_slot(k, q_own, *buf_a)

    for e in range(1, n_pa):
        u_copy(e).wait_recv()
    column = lax.broadcasted_iota(jnp.int32, (slots, m_all), 1)
    picked = jnp.zeros((slots, n_pb * q_count), F32)
    for e in range(n_pa):
        shard = (o - e + n_pa) % n_pa
        one_hot = (held == column + (shard - b) * pd) & (column >= b * pd) & (column < (b + 1) * pd)
        one_hot = jnp.where(one_hot, 1.0, 0.0).astype(BF16)
        table = t_buf[e, :, :, 0:m_all].reshape(n_pb * q_count, m_all)
        for part in three_parts(table):
            picked = picked + nt_dot(one_hot, part)
    picked_parts = jnp.concatenate([p.astype(F32) for p in three_parts(picked)], axis=0).astype(BF16)
    row_at = lax.broadcasted_iota(jnp.int32, (n_pb * q_count, rows), 0)
    lane_at = lax.broadcasted_iota(jnp.int32, (n_pb * q_count, rows), 1)
    for d in range(n_pb):
        spread = jnp.where(row_at == d * q_count + lane_at // tokens, 1.0, 0.0).astype(BF16)
        wide = nn_dot(picked_parts, spread)
        t_exp[d] = wide[0:slots] + wide[slots:2 * slots] + wide[2 * slots:3 * slots]

    beside(n_pb - 1, buf_b, 0, buf_a)
    dq_own[...] = query_grad(0)

    def two_groups(i, carry):
        d = n_pb - 2 - 2 * i
        beside(d, buf_a, d + 1, buf_b)
        send_grad(d + 1)
        beside(d - 1, buf_b, d, buf_a)
        send_grad(d)
        return carry

    lax.fori_loop(0, (n_pb - 2) // 2, two_groups, 0)
    factor = factor_of(1, lse_b, inv_b)
    for k in range(slots):
        grad_slot(k, 1, factor, prob_b)
    send_grad(1)

    def passage_grad(c):
        part = pl.ds(c * chunk * length, chunk * length)
        q_all = q_buf[...].reshape(n_pb * rows, q_ref.shape[1])
        slot_grad = nn_dot(coef[part, :], q_all).astype(BF16).astype(F32)
        unit_c = unit[part, :]
        inner = jnp.sum(unit_c * slot_grad, axis=1, keepdims=True)
        pg_ref[part, :] = ((slot_grad - unit_c * inner) * scale[part, :]).astype(BF16)

    for c in range(chunks // 4):
        passage_grad(c)
    total = dq_own[...]
    for d in range(n_pb - 1, 0, -1):
        d_copy(d).wait_recv()
        total = total + dq_in[d].astype(F32)
    sum_out[...] = jnp.transpose(total).astype(BF16)
    for e in range(1, n_pa):
        s_copy(e).start()
    for c in range(chunks // 4, chunks):
        passage_grad(c)
    mine = sum_out[pl.ds(pl.multiple_of(o * piece, piece), piece), :].astype(F32)
    for e in range(1, n_pa):
        s_copy(e).wait_recv()
        mine = mine + sum_in[e].astype(F32)
    qg_ref[...] = mine

    for d in range(1, n_pb):
        t_copy(d).wait_send()
        q_copy(d).wait_send()
        d_copy(d).wait_send()
    for e in range(1, n_pa):
        u_copy(e).wait_send()
        s_copy(e).wait_send()


def solution(mesh):
    n_pb, n_pa = mesh.shape["pb"], mesh.shape["pa"]

    def on_device(queries, encoder_outputs, proj_weight, bm25_rank, dense_rank, custodian):
        _, slots, length, hidden = encoder_outputs.shape
        dim = proj_weight.shape[1]
        rows = queries.shape[0]
        q_count, _, m_all = bm25_rank.shape
        pd = m_all // n_pb
        tokens = rows // q_count
        all_rows = slots * length
        piece = rows // n_pa
        vmem = pl.BlockSpec(memory_space=pltpu.VMEM)
        dma = pltpu.SemaphoreType.DMA
        proj_grad, query_grad = pl.pallas_call(
            functools.partial(step_kernel, n_pb, n_pa, slots, length, pd, tokens),
            out_shape=(
                jax.ShapeDtypeStruct((all_rows, dim), BF16),
                jax.ShapeDtypeStruct((piece, dim), F32),
            ),
            in_specs=[pl.BlockSpec(memory_space=pl.ANY)] * 6,
            out_specs=(vmem, vmem),
            scratch_shapes=[
                pltpu.VMEM((all_rows, hidden), BF16),
                pltpu.VMEM((hidden, dim), BF16),
                pltpu.VMEM((q_count, m_all), jnp.int32),
                pltpu.VMEM((q_count, m_all), jnp.int32),
                pltpu.VMEM((1, slots), jnp.int32),
                pltpu.VMEM((all_rows, dim), F32),
                pltpu.VMEM((all_rows, 1), F32),
                pltpu.VMEM((all_rows, dim), BF16),
                pltpu.VMEM((dim, all_rows), BF16),
                pltpu.VMEM((all_rows, rows), F32),
                pltpu.VMEM((all_rows, rows), F32),
                pltpu.VMEM((all_rows, n_pb * rows), BF16),
                pltpu.VMEM((slots, rows), F32),
                pltpu.VMEM((slots, rows), F32),
                pltpu.VMEM((slots, rows), F32),
                pltpu.VMEM((slots, rows), F32),
                pltpu.VMEM((n_pb, rows, dim), BF16),
                pltpu.VMEM((n_pa, n_pb, q_count, max(128, m_all)), F32),
                pltpu.VMEM((n_pb, slots, rows), F32),
                pltpu.VMEM((dim, rows), F32),
                pltpu.VMEM((n_pb, dim, rows), BF16),
                pltpu.VMEM((n_pb, dim, rows), BF16),
                pltpu.VMEM((rows, dim), BF16),
                pltpu.VMEM((n_pa, piece, dim), BF16),
                dma((slots,)), dma((5,)),
                dma((n_pb,)), dma((n_pb,)),
                dma((n_pb,)), dma((n_pb,)),
                dma((n_pa,)), dma((n_pa,)),
                dma((n_pb,)), dma((n_pb,)),
                dma((n_pa,)), dma((n_pa,)),
            ],
            compiler_params=pltpu.CompilerParams(collective_id=0, has_side_effects=True),
        )(
            queries, encoder_outputs.reshape(all_rows, hidden), proj_weight,
            bm25_rank[:, 0, :], dense_rank[:, 0, :], custodian,
        )
        hid_grad = lax.dot_general(
            proj_grad, proj_weight, (((1,), (1,)), ((), ())), preferred_element_type=F32)
        return query_grad, hid_grad.astype(BF16).reshape(1, slots, length, hidden)

    return jax.shard_map(
        on_device,
        mesh=mesh,
        in_specs=(
            P("pb", None),
            P("pb", "pa", None, None),
            P(),
            P("pb", "pa", None),
            P("pb", "pa", None),
            P("pb", "pa"),
        ),
        out_specs=(P(("pb", "pa"), None), P("pb", "pa", None, None)),
        check_vma=False,
    )
```

```python
import functools
import math

import jax
import jax.numpy as jnp
from jax import lax
from jax.experimental import pallas as pl
from jax.experimental.pallas import tpu as pltpu
from jax.sharding import PartitionSpec as P

DEPTH = 100

tau = 0.05
inv_temp = 20.0
rrf_offset = 60.0
norm_eps = 1e-06

MESH = pl.DeviceIdType.MESH
F32 = jnp.float32
BF16 = jnp.bfloat16


def joined_target(bm25_rank, dense_rank):
    first = jnp.where(bm25_rank < DEPTH, rrf_offset / (rrf_offset + bm25_rank.astype(F32)), 0.0)
    second = jnp.where(dense_rank < DEPTH, rrf_offset / (rrf_offset + dense_rank.astype(F32)), 0.0)
    return first + second


def xor(a, b, size):
    total = 0
    bit = 1
    while bit < size:
        total = total + ((a // bit + b // bit) % 2) * bit
        bit *= 2
    return total


def three_parts(x):
    first = x.astype(BF16)
    rest = x - first.astype(F32)
    second = rest.astype(BF16)
    third = (rest - second.astype(F32)).astype(BF16)
    return first, second, third


def nt_dot(a, b):
    return lax.dot_general(a, b, (((1,), (1,)), ((), ())), preferred_element_type=F32)


def nn_dot(a, b):
    return jnp.dot(a, b, preferred_element_type=F32)


def step_kernel(
    n_pb, n_pa, slots, length, pd, tokens,
    q_ref, x_ref, w_ref, bm_ref, de_ref, idx_ref,
    pg_ref, qg_ref,
    x_buf, w_buf, bm_buf, de_buf, idx_buf,
    unit, scale, emb, emb_t, prob, coef, lse_buf, inv_buf,
    q_buf, t_buf, t_own, t_exp, dq_keep, dq_out, dq_part, dq_in, sum_out, sum_in,
    x_sem, i_sem, q_send, q_recv, t_send, t_recv, u_send, u_recv, p_send, p_recv, d_send, d_recv, s_send, s_recv,
):
    b = lax.axis_index("pb")
    o = lax.axis_index("pa")
    rows = q_ref.shape[0]
    q_count, m_all = bm_ref.shape
    piece = rows // n_pa
    chunk = 4 if slots % 4 == 0 else 1

    def x_copy(k):
        part = pl.ds(k * length, length)
        return pltpu.make_async_copy(x_ref.at[part], x_buf.at[part], x_sem.at[k])

    def q_copy(d):
        return pltpu.make_async_remote_copy(
            q_buf.at[d - 1 if d % 2 else 0], q_buf.at[d], q_send.at[d], q_recv.at[d],
            device_id={"pb": xor(b, 1 if d % 2 else d, n_pb)}, device_id_type=MESH)

    def t_copy(d):
        return pltpu.make_async_remote_copy(
            t_buf.at[0], t_buf.at[d], t_send.at[d], t_recv.at[d],
            device_id={"pb": xor(b, d, n_pb)}, device_id_type=MESH)

    def u_copy(e):
        return pltpu.make_async_remote_copy(
            t_own.at[0], t_own.at[e], u_send.at[e], u_recv.at[e],
            device_id={"pa": (o + e) % n_pa}, device_id_type=MESH)

    def p_copy(d):
        h = d // 2
        return pltpu.make_async_remote_copy(
            dq_out.at[d], dq_part.at[h], p_send.at[h], p_recv.at[h],
            device_id={"pb": xor(b, 1, n_pb)}, device_id_type=MESH)

    def d_copy(d):
        h = d // 2
        return pltpu.make_async_remote_copy(
            dq_out.at[d], dq_in.at[h], d_send.at[h], d_recv.at[h],
            device_id={"pb": xor(b, d, n_pb)}, device_id_type=MESH)

    def s_copy(e):
        to = (o + e) % n_pa
        return pltpu.make_async_remote_copy(
            sum_out.at[pl.ds(pl.multiple_of(to * piece, piece), piece)],
            sum_in.at[e], s_send.at[e], s_recv.at[e],
            device_id={"pa": to}, device_id_type=MESH)

    barrier = pltpu.get_barrier_semaphore()
    for d in range(1, n_pb):
        pl.semaphore_signal(barrier, inc=1, device_id={"pb": xor(b, d, n_pb)}, device_id_type=MESH)
    for e in range(1, n_pa):
        pl.semaphore_signal(barrier, inc=1, device_id={"pa": (o + e) % n_pa}, device_id_type=MESH)

    small = [
        pltpu.make_async_copy(src, dst, i_sem.at[n])
        for n, (src, dst) in enumerate((
            (w_ref, w_buf), (q_ref, q_buf.at[0]), (bm_ref, bm_buf), (de_ref, de_buf),
            (idx_ref, idx_buf)))
    ]
    small[2].start()
    small[3].start()
    small[0].start()
    for k in range(slots):
        x_copy(k).start()
        if k == chunk - 1:
            small[1].start()
            small[4].start()

    def project(c):
        part = pl.ds(c * chunk * length, chunk * length)
        for k in range(c * chunk, (c + 1) * chunk):
            x_copy(k).wait()
        projected = nn_dot(x_buf[part, :], w_buf[...])
        scaling = lax.rsqrt(jnp.sum(projected * projected, axis=1, keepdims=True) + norm_eps)
        unit_c = projected * scaling
        unit[part, :] = unit_c
        scale[part, :] = scaling
        emb[part, :] = unit_c.astype(BF16)
        emb_t[:, part] = jnp.transpose(unit_c).astype(BF16)

    def send_first():
        pl.semaphore_wait(barrier, n_pb + n_pa - 2)
        for d in range(1, n_pb):
            t_copy(d).start()
        q_copy(1).start()
        for d in range(n_pb - 2, 0, -2):
            q_copy(d).start()

    def send_second():
        for d in range(1, n_pb):
            t_copy(d).wait_recv()
        row = lax.broadcasted_iota(jnp.int32, (pd, m_all), 0)
        at = lax.broadcasted_iota(jnp.int32, (pd, m_all), 1)
        pick = jnp.where(at == row + b * pd, 1.0, 0.0).astype(BF16)
        table = t_buf[:, :, 0:m_all].reshape(n_pb * q_count, m_all)
        first, second, third = three_parts(table)
        t_own[0, :, 0:n_pb * q_count] = nt_dot(pick, first) + nt_dot(pick, second) + nt_dot(pick, third)
        for e in range(1, n_pa):
            u_copy(e).start()

    small[2].wait()
    small[3].wait()
    t_buf[0, :, 0:m_all] = joined_target(bm_buf[...], de_buf[...])
    small[0].wait()
    chunks = slots // chunk
    first_at = max(chunks - 2, 0)
    for c in range(chunks):
        project(c)
        if c == first_at:
            small[1].wait()
            small[4].wait()
            send_first()

    same_query = jnp.where(
        lax.broadcasted_iota(jnp.int32, (rows, rows), 0) // tokens
        == lax.broadcasted_iota(jnp.int32, (rows, rows), 1) // tokens, 1.0, 0.0).astype(BF16)
    across = jnp.broadcast_to(idx_buf[...], (slots, slots))
    on_diagonal = lax.broadcasted_iota(jnp.int32, (slots, slots), 0) == lax.broadcasted_iota(
        jnp.int32, (slots, slots), 1)
    held = jnp.sum(jnp.where(on_diagonal, across, 0).astype(F32), axis=1, keepdims=True)
    held = held.astype(jnp.int32)
    filled = held >= 0

    def score_slot(k, q_rows, prob, lse, inv):
        part = pl.ds(k * length, length)
        raw = nt_dot(emb[part, :], q_rows)
        largest = jnp.max(raw, axis=0, keepdims=True)
        power = jnp.exp2((raw - largest) * (inv_temp * math.log2(math.e)))
        total = jnp.sum(power, axis=0, keepdims=True)
        prob[part, :] = power
        lse[pl.ds(k, 1), :] = largest * inv_temp + jnp.log(total)
        inv[pl.ds(k, 1), :] = 1.0 / total

    def factor_of(d, lse, inv):
        first, second, third = three_parts(lse[...])
        score = nn_dot(first, same_query) + nn_dot(second, same_query) + nn_dot(third, same_query)
        residual = (score * (tau / tokens) - t_exp[d]).astype(BF16).astype(F32)
        return jnp.where(filled, residual * (1.0 / tokens) * inv[...], 0.0)

    def spread_targets():
        for e in range(1, n_pa):
            u_copy(e).wait_recv()
        row = lax.broadcasted_iota(jnp.int32, (slots, pd), 1)
        picked = jnp.zeros((slots, n_pb * q_count), F32)
        for e in range(n_pa):
            shard = (o - e + n_pa) % n_pa
            one_hot = jnp.where(held == row + shard * pd, 1.0, 0.0).astype(BF16)
            for part in three_parts(t_own[e, :, 0:n_pb * q_count]):
                picked = picked + nn_dot(one_hot, part)
        picked_parts = jnp.concatenate(
            [p.astype(F32) for p in three_parts(picked)], axis=0).astype(BF16)
        row_at = lax.broadcasted_iota(jnp.int32, (n_pb * q_count, rows), 0)
        lane_at = lax.broadcasted_iota(jnp.int32, (n_pb * q_count, rows), 1)
        for d in range(n_pb):
            spread = jnp.where(row_at == d * q_count + lane_at // tokens, 1.0, 0.0).astype(BF16)
            wide = nn_dot(picked_parts, spread)
            t_exp[d] = wide[0:slots] + wide[slots:2 * slots] + wide[2 * slots:3 * slots]

    order = [0, 1]
    for d in range(n_pb - 2, 2, -2):
        order += [d, d + 1]
    order += [3, 2]
    lag = prob.shape[0] - 1

    def scores(i):
        d = order[i]
        if d % 2 and d != 3:
            q_copy(d).wait_recv()
        elif d >= 4:
            q_copy(d).wait_recv()
            q_copy(d + 1).start()
        elif d == 3:
            if i == 2:
                q_copy(2).wait_recv()
                q_copy(3).start()
            q_copy(3).wait_recv()
        if i > 2 and i == n_pb - 3:
            q_copy(2).wait_recv()
            q_copy(3).start()
        slot = i % (lag + 1)
        q_rows = q_buf[d]
        for k in range(slots):
            score_slot(k, q_rows, prob.at[slot], lse_buf.at[slot], inv_buf.at[slot])

    def finish_pair(d):
        p_copy(d + 1).wait_recv()
        dq_out[d] = (dq_keep[d // 2] + dq_part[d // 2].astype(F32)).astype(BF16)
        d_copy(d).start()

    def grads(i):
        d = order[i]
        slot = i % (lag + 1)
        factor = factor_of(d, lse_buf.at[slot], inv_buf.at[slot])
        lanes = pl.ds(d * rows, rows)
        for k in range(slots):
            part = pl.ds(k * length, length)
            coef[part, lanes] = (prob[slot, part, :] * factor[k:k + 1, :]).astype(BF16)
        dq = nn_dot(emb_t[...], coef[:, lanes])
        if d % 2:
            dq_out[d] = dq.astype(BF16)
            p_copy(d).start()
        else:
            dq_keep[d // 2] = dq
        before = order[i - 1]
        if i > 2 and before % 2 and before > 3:
            finish_pair(before - 1)

    for i in range(n_pb + lag):
        if i < n_pb:
            scores(i)
        if i == 1:
            send_second()
        if i == lag:
            spread_targets()
        if i >= lag:
            grads(i - lag)
    finish_pair(2)

    def passage_grad(c):
        part = pl.ds(c * chunk * length, chunk * length)
        q_all = q_buf[...].reshape(n_pb * rows, q_ref.shape[1])
        slot_grad = nn_dot(coef[part, :], q_all).astype(BF16).astype(F32)
        unit_c = unit[part, :]
        inner = jnp.sum(unit_c * slot_grad, axis=1, keepdims=True)
        pg_ref[part, :] = ((slot_grad - unit_c * inner) * scale[part, :]).astype(BF16)

    for c in range(chunks // 2):
        passage_grad(c)
    p_copy(1).wait_recv()
    total = dq_keep[0] + dq_part[0].astype(F32)
    for d in range(n_pb - 2, 0, -2):
        d_copy(d).wait_recv()
        total = total + dq_in[d // 2].astype(F32)
    sum_out[...] = jnp.transpose(total).astype(BF16)
    for e in range(1, n_pa):
        s_copy(e).start()
    for c in range(chunks // 2, chunks):
        passage_grad(c)
    mine = sum_out[pl.ds(pl.multiple_of(o * piece, piece), piece), :].astype(F32)
    for e in range(1, n_pa):
        s_copy(e).wait_recv()
        mine = mine + sum_in[e].astype(F32)
    qg_ref[...] = mine

    for d in range(1, n_pb):
        t_copy(d).wait_send()
        q_copy(d).wait_send()
        if d % 2:
            p_copy(d).wait_send()
        else:
            d_copy(d).wait_send()
    for e in range(1, n_pa):
        u_copy(e).wait_send()
        s_copy(e).wait_send()


def solution(mesh):
    n_pb, n_pa = mesh.shape["pb"], mesh.shape["pa"]

    def on_device(queries, encoder_outputs, proj_weight, bm25_rank, dense_rank, custodian):
        _, slots, length, hidden = encoder_outputs.shape
        dim = proj_weight.shape[1]
        rows = queries.shape[0]
        q_count, _, m_all = bm25_rank.shape
        pd = m_all // n_pb
        tokens = rows // q_count
        all_rows = slots * length
        piece = rows // n_pa
        half = n_pb // 2
        held = 5
        vmem = pl.BlockSpec(memory_space=pltpu.VMEM)
        dma = pltpu.SemaphoreType.DMA
        proj_grad, query_grad = pl.pallas_call(
            functools.partial(step_kernel, n_pb, n_pa, slots, length, pd, tokens),
            out_shape=(
                jax.ShapeDtypeStruct((all_rows, dim), BF16),
                jax.ShapeDtypeStruct((piece, dim), F32),
            ),
            in_specs=[pl.BlockSpec(memory_space=pl.ANY)] * 6,
            out_specs=(vmem, vmem),
            scratch_shapes=[
                pltpu.VMEM((all_rows, hidden), BF16),
                pltpu.VMEM((hidden, dim), BF16),
                pltpu.VMEM((q_count, m_all), jnp.int32),
                pltpu.VMEM((q_count, m_all), jnp.int32),
                pltpu.VMEM((1, slots), jnp.int32),
                pltpu.VMEM((all_rows, dim), F32),
                pltpu.VMEM((all_rows, 1), F32),
                pltpu.VMEM((all_rows, dim), BF16),
                pltpu.VMEM((dim, all_rows), BF16),
                pltpu.VMEM((held, all_rows, rows), F32),
                pltpu.VMEM((all_rows, n_pb * rows), BF16),
                pltpu.VMEM((held, slots, rows), F32),
                pltpu.VMEM((held, slots, rows), F32),
                pltpu.VMEM((n_pb, rows, dim), BF16),
                pltpu.VMEM((n_pb, q_count, max(128, m_all)), F32),
                pltpu.VMEM((n_pa, pd, max(128, n_pb * q_count)), F32),
                pltpu.VMEM((n_pb, slots, rows), F32),
                pltpu.VMEM((half, dim, rows), F32),
                pltpu.VMEM((n_pb, dim, rows), BF16),
                pltpu.VMEM((half, dim, rows), BF16),
                pltpu.VMEM((half, dim, rows), BF16),
                pltpu.VMEM((rows, dim), BF16),
                pltpu.VMEM((n_pa, piece, dim), BF16),
                dma((slots,)), dma((5,)),
                dma((n_pb,)), dma((n_pb,)),
                dma((n_pb,)), dma((n_pb,)),
                dma((n_pa,)), dma((n_pa,)),
                dma((half,)), dma((half,)),
                dma((half,)), dma((half,)),
                dma((n_pa,)), dma((n_pa,)),
            ],
            compiler_params=pltpu.CompilerParams(collective_id=0, has_side_effects=True),
        )(
            queries, encoder_outputs.reshape(all_rows, hidden), proj_weight,
            bm25_rank[:, 0, :], dense_rank[:, 0, :], custodian,
        )
        hid_grad = lax.dot_general(
            proj_grad, proj_weight, (((1,), (1,)), ((), ())), preferred_element_type=F32)
        return query_grad, hid_grad.astype(BF16).reshape(1, slots, length, hidden)

    return jax.shard_map(
        on_device,
        mesh=mesh,
        in_specs=(
            P("pb", None),
            P("pb", "pa", None, None),
            P(),
            P("pb", "pa", None),
            P("pb", "pa", None),
            P("pb", "pa"),
        ),
        out_specs=(P(("pb", "pa"), None), P("pb", "pa", None, None)),
        check_vma=False,
    )
```
